512 devices in a mesh: role: 4 (over y), pairs: 128 (over x, z, core).
Axes of the slice: x: 4, y: 4, z: 16, core: 2. Of those that a mesh axis runs over, the one named last changes fastest.
Arguments:
- three_index: bfloat16 [256, 1024, 512], P('pairs'), may hold values from -6 to 6
- coeff: bfloat16 [512, 512, 256], P('pairs'), may hold values from -6 to 6
- amps: bfloat16 [512, 256, 256], P('pairs'), may hold values from -4 to 4
- eps_virt: float32 [512, 256], P('pairs'), may hold values from 0.3 to 3
- eps_occ: float32 [256], replicated, may hold values from -1.5 to -0.3
- nvirt: int32 [512], P('pairs'), may hold values from 64 to 256, as said below
- pair_occ: int32 [512, 2], P('pairs'), may hold values from 0 to 255, as said below
- partners: int32 [512, 8], P('pairs'), may hold values from 0 to 511, as said below
- coupling: float32 [512, 8], P('pairs'), may hold values from -1 to 1
- pair_owner: int32 [512], P('pairs'), may hold values from 1 to 3, as said below
Outputs:
- amps_out: bfloat16 [1024, 256, 256], P(('role', 'pairs'))
- dressed_out: bfloat16 [1024, 512, 256], P(('role', 'pairs'))
The draws below stay inside these ranges and needn't reach their ends.
Inputs may be any that keep to these rules, and one draw needn't show every extreme that they name: `nvirt`: each block of 4 consecutive pairs has one pair with all 256 virtuals. `pair_occ`: for pair k in block c = k // 4, the first orbital is one of the 2 orbitals numbered from 2 * c, and the second is one of the 6 orbitals numbered cyclically from 2 * (c - 1) modulo 256. Pair k's partners are distinct pairs of its own block of 4 pairs and the blocks just before and after it, cyclically modulo 512. `pair_owner`: in each block of 4 consecutive pairs, each of the roles 1 to 3 holds one or two pairs and exactly one role holds two.
All inputs are finite; a program needn't handle non-finite values.
Results may differ from the reference program's by a relative error of at most 0.012.
Values may be sent and summed in bfloat16 or wider, within the bound.
A program may use at most 64 MiB of HBM per device.

```python
import math
import jax
import jax.numpy as jnp
from jax import lax

NAUX = 1024
NPAO = 512
NV = 256
PARTNERS = 8
ITERS = 2
O_COL = 2
P_COL = 4
SLOTS = 2
NOCC = 256
PAIRS = 512
SLOT_ALL = 1024
N_PAIRS = 128


def draw_nvirt(key, part):
    column_count = PAIRS // P_COL
    counts = jax.random.randint(jax.random.fold_in(key, 101), (column_count, P_COL), NV // 4, NV + 1, dtype=jnp.int32)
    full_at = jax.random.randint(jax.random.fold_in(key, 102), (column_count, 1), 0, P_COL, dtype=jnp.int32)
    places = jnp.arange(P_COL, dtype=jnp.int32)[None, :]
    counts = jnp.where(places == full_at, NV, counts)
    return counts.reshape(PAIRS).astype(jnp.int32)


def draw_pair_occ(key, part):
    column_count = PAIRS // P_COL
    own = O_COL * jnp.arange(column_count, dtype=jnp.int32)
    picks = jax.random.randint(jax.random.fold_in(key, 201), (column_count, 6), 0, O_COL, dtype=jnp.int32)
    side_pick = picks[:, 5] % 2
    first_a = own + picks[:, 0]
    second_a = own - O_COL + picks[:, 1]
    first_b = own + picks[:, 2]
    second_b = own + O_COL + picks[:, 3]
    first_c = own + 1 - jnp.where(side_pick == 0, picks[:, 0], picks[:, 2])
    second_c = own + jnp.where(side_pick == 0, -O_COL, O_COL) + picks[:, 4]
    firsts = jnp.stack([own, first_a, first_b, first_c], axis=1)
    seconds = jnp.stack([own + 1, second_a, second_b, second_c], axis=1)
    seconds = jnp.mod(seconds, NOCC)
    return jnp.stack([firsts, seconds], axis=2).reshape(PAIRS, 2).astype(jnp.int32)


def draw_partners(key, part):
    column_count = PAIRS // P_COL
    pair_ids = jnp.arange(PAIRS, dtype=jnp.int32)
    columns = pair_ids // P_COL
    nearby = jnp.arange(3 * P_COL, dtype=jnp.int32)
    scores = jax.random.randint(jax.random.fold_in(key, 301), (PAIRS, 3 * P_COL), 0, 1 << 20, dtype=jnp.int32) * (3 * P_COL) + nearby[None, :]
    chosen = jnp.argsort(scores, axis=1)[:, :PARTNERS].astype(jnp.int32)
    block_ids = jnp.mod(columns[:, None] - 1 + chosen // P_COL, column_count)
    return (block_ids * P_COL + chosen % P_COL).astype(jnp.int32)


def draw_pair_owner(key, part):
    column_count = PAIRS // P_COL
    extra = jax.random.randint(jax.random.fold_in(key, 401), (column_count, 1), 1, 4, dtype=jnp.int32)
    basic = jnp.broadcast_to(jnp.array([1, 2, 3], jnp.int32)[None, :], (column_count, 3))
    owners = jnp.concatenate([basic, extra], axis=1)
    scores = jax.random.randint(jax.random.fold_in(key, 402), (column_count, 4), 0, 1 << 20, dtype=jnp.int32) * 4 + jnp.arange(4, dtype=jnp.int32)[None, :]
    order = jnp.argsort(scores, axis=1)
    owners = jnp.take_along_axis(owners, order, axis=1)
    return owners.reshape(PAIRS).astype(jnp.int32)


def levels(stream_key, shape, shards, low, top_value):
    loudness, own = 1.0, jax.random.fold_in(stream_key, 6)
    for axis_at, parts in shards:
        draws = jnp.exp(jax.random.uniform(jax.random.fold_in(own, axis_at), (parts,), jnp.float32, low / len(shards), top_value / len(shards)))
        loudness = loudness * jnp.repeat(draws, shape[axis_at] // parts).reshape([-1 if axis == axis_at else 1 for axis in range(len(shape))])
    return loudness


def noise(rng, dims, width, limit, split=(), held_as=jnp.bfloat16):
    values = width * jax.random.normal(rng, dims, jnp.float32)
    if split:
        values = values * levels(rng, dims, split, -0.22, 0.18)
    return jnp.clip(values, -limit, limit).astype(held_as)


def setup_inputs(seed: int = 0) -> dict:
    key_of = jax.random.split(jax.random.key(seed), 11)
    three_index = noise(key_of[0], (NOCC, NAUX, NPAO), 1.0, 6.0, ((0, 128),))
    coeff = noise(key_of[1], (PAIRS, NPAO, NV), 1.0, 6.0, ((0, 128),))
    amps = noise(key_of[2], (PAIRS, NV, NV), 0.5, 4.0, ((0, 128),))
    eps_virt = jnp.clip(jnp.exp(math.log(3.0) - 2.3025851 * jax.random.uniform(key_of[3], (PAIRS, NV), jnp.float32) ** levels(key_of[3], (PAIRS, NV), ((0, 128),), -0.2, 0.2)), 0.3, 3.0)
    eps_occ = jnp.clip(jax.random.uniform(key_of[4], (NOCC,), jnp.float32, -1.5, -0.3), -1.5, -0.3)
    nvirt = draw_nvirt(jax.random.fold_in(key_of[10], 71), 0)
    pair_occ = draw_pair_occ(jax.random.fold_in(key_of[10], 71), 0)
    partners = draw_partners(jax.random.fold_in(key_of[10], 71), 0)
    coupling = jnp.clip(jax.random.uniform(key_of[8], (PAIRS, PARTNERS), jnp.float32, -1.0, 1.0) * levels(key_of[8], (PAIRS, PARTNERS), ((0, 128),), -0.4, 0.0), -1.0, 1.0)
    pair_owner = draw_pair_owner(jax.random.fold_in(key_of[10], 71), 0)
    return dict(three_index=three_index, coeff=coeff, amps=amps, eps_virt=eps_virt, eps_occ=eps_occ, nvirt=nvirt, pair_occ=pair_occ, partners=partners, coupling=coupling, pair_owner=pair_owner)


def slot_numbers(pair_owner):
    owners = pair_owner.reshape(-1, P_COL)
    same_owner = (owners[:, :, None] == owners[:, None, :]).astype(jnp.int32)
    earlier = jnp.tril(jnp.ones((P_COL, P_COL), jnp.int32), -1)
    pair_ranks = lax.optimization_barrier(jnp.sum(same_owner * earlier[None, :, :], axis=2))
    columns = jnp.arange(owners.shape[0], dtype=jnp.int32)[:, None]
    return ((owners * N_PAIRS + columns) * SLOTS + pair_ranks).reshape(-1).astype(jnp.int32)

def reference(three_index, coeff, amps, eps_virt, eps_occ, nvirt, pair_occ, partners, coupling, pair_owner):
    pao_scale = 1.0 / math.sqrt(NPAO)
    aux_scale = 1.0 / math.sqrt(NAUX)
    virt_scale = 1.0 / math.sqrt(NV)
    virtuals = jnp.arange(NV, dtype=jnp.int32)
    pair_ids = jnp.arange(PAIRS, dtype=jnp.int32)

    def integral(packed):
        pair_at, orbitals = packed
        first_half = (jnp.dot(three_index[pair_occ[pair_at, 0]], orbitals, preferred_element_type=jnp.float32) * pao_scale).astype(jnp.bfloat16)
        second_half = (jnp.dot(three_index[pair_occ[pair_at, 1]], orbitals, preferred_element_type=jnp.float32) * pao_scale).astype(jnp.bfloat16)
        return (jnp.dot(first_half.T, second_half, preferred_element_type=jnp.float32) * aux_scale).astype(jnp.bfloat16)

    def update(packed, current):
        pair_at, pair_int = packed
        partner_ids = partners[pair_at]
        own_orb = coeff[pair_at].astype(jnp.float32)
        partner_orb = coeff[partner_ids].astype(jnp.float32)
        intersection = (jnp.einsum('mb,kmc->kbc', own_orb, partner_orb) * (1.0 / NPAO)).astype(jnp.bfloat16)
        partner_amp = current[partner_ids].astype(jnp.float32)
        middle = jnp.einsum('kbc,kcd->kbd', intersection.astype(jnp.float32), partner_amp).astype(jnp.bfloat16)
        partner_terms = jnp.einsum('kbd,ked->kbe', middle.astype(jnp.float32), intersection.astype(jnp.float32))
        coupled = lax.optimization_barrier(jnp.sum(coupling[pair_at][:, None, None] * partner_terms, axis=0))
        occ_shift = eps_occ[pair_occ[pair_at, 0]] + eps_occ[pair_occ[pair_at, 1]]
        energy = eps_virt[pair_at][:, None] + eps_virt[pair_at][None, :] - occ_shift
        own_amp = current[pair_at].astype(jnp.float32)
        fresh_amp = own_amp - (pair_int.astype(jnp.float32) + energy * own_amp + coupled) / (energy + 1.0)
        keep_rows = (virtuals < nvirt[pair_at]).astype(jnp.float32)
        fresh_amp = (fresh_amp * keep_rows[:, None] * keep_rows[None, :]).astype(jnp.bfloat16)
        dressed = (coeff[pair_at].astype(jnp.float32) + jnp.dot(coeff[pair_at], fresh_amp, preferred_element_type=jnp.float32) * virt_scale).astype(jnp.bfloat16)
        return (fresh_amp, dressed)
    current_amp = amps
    current_orb = coeff
    for iteration in range(ITERS):
        pair_ints = lax.map(integral, (pair_ids, current_orb))
        held_amp = current_amp
        current_amp, current_orb = lax.map(lambda packed: update(packed, held_amp), (pair_ids, pair_ints))
    slot_ids = slot_numbers(pair_owner)
    amps_out = jnp.zeros((SLOT_ALL, NV, NV), jnp.bfloat16).at[slot_ids].set(current_amp)
    dressed_out = jnp.zeros((SLOT_ALL, NPAO, NV), jnp.bfloat16).at[slot_ids].set(current_orb)
    return (amps_out, dressed_out)
```

```python
import functools
import math

import jax
import jax.numpy as jnp
from jax import lax
from jax.experimental import pallas as pl
from jax.experimental.pallas import tpu as pltpu
from jax.sharding import PartitionSpec as P

SLOTS = 2
MESH = pl.DeviceIdType.MESH
BF = jnp.bfloat16
F32 = jnp.float32

OCC, PART, COUP, XM, YM, CM, T1D, T1F, C2M, T2D, T2F, COUNT = 0, 2, 4, 6, 10, 14, 16, 20, 24, 28, 32, 36


def dot(a, b):
    return jnp.dot(a, b, preferred_element_type=F32)


def dot_nt(a, b):
    return lax.dot_general(a, b, (((1,), (1,)), ((), ())), preferred_element_type=F32)


def kernel(
    n, roles,
    three_hbm, coeff_hbm, amps_hbm, occ_hbm, part_hbm, coup_hbm,
    ev_ref, eo_ref, nv_ref, occ_ref, part_ref, coup_ref, own_ref,
    out_amp, out_orb,
    b_v, a_v, t_v, x_in, y_out, y_left, y_right, yit_v, s_v, u_v, c_out, c_in, c_own, rm_v, k_v,
    t1_v, t1_f, c2_out, c2_in, t2_v,
    occ_in, part_in, coup_in,
    load_sem, send_sem, recv_sem,
):
    r = lax.axis_index("role")
    c = lax.axis_index("pairs")
    up, down = lax.rem(r + 1, roles), lax.rem(r + roles - 1, roles)
    naux, npao = b_v.shape[1], b_v.shape[2]
    nv = a_v.shape[2]
    hw = nv // 2
    hr = nv // 2
    pao_scale = 1.0 / math.sqrt(npao)
    aux_scale = 1.0 / math.sqrt(naux)
    virt_scale = 1.0 / math.sqrt(nv)
    y_in = (y_left, y_right)
    near = lax.rem(c, 2)

    def remote(src, dst, base, s_at, r_at, device):
        return pltpu.make_async_remote_copy(
            src_ref=src, dst_ref=dst,
            send_sem=send_sem.at[base + s_at], recv_sem=recv_sem.at[base + r_at],
            device_id=device, device_id_type=MESH,
        )

    def side(d):
        return (r, lax.rem(c + 2 * d - 1 + n, n))

    def level(v):
        return (lax.rem(r + 1 + 2 * v, roles), c)

    def meta(d):
        return (
            remote(occ_hbm, occ_in.at[1 - d], OCC, d, 1 - d, side(d)),
            remote(part_hbm, part_in.at[1 - d], PART, d, 1 - d, side(d)),
            remote(coup_hbm, coup_in.at[1 - d], COUP, d, 1 - d, side(d)),
        )

    def xmsg(d, h):
        cols = pl.ds(h * hw, hw)
        return remote(coeff_hbm.at[r, :, cols], x_in.at[1 - d, :, cols], XM, 2 * d + h, 2 * (1 - d) + h, side(d))

    def ymsg(d, h):
        return remote(y_out.at[d, h], y_in[h].at[2 * (1 - d)], YM, 2 * d + h, 2 * (1 - d) + h, side(d))

    def cmsg(d):
        return remote(c_out.at[d], c_in.at[1 - d], CM, d, 1 - d, side(d))

    def c2msg(d, h):
        return remote(c2_out.at[d, h], c2_in.at[1 - d, h], C2M, 2 * d + h, 2 * (1 - d) + h, side(d))

    def direct(buf, base, v, h):
        return remote(buf.at[r, h], buf.at[r, h], base, 2 * v + h, 2 * (1 - v) + h, level(v))

    def forward(buf, base, v, h):
        which = down if v == 0 else up
        part = buf.at[which, h, pl.ds(v * hr, hr)]
        return remote(part, part, base, 2 * v + h, 2 * (1 - v) + h, level(v))

    load_a = pltpu.make_async_copy(coeff_hbm, a_v, load_sem.at[0])
    load_b = pltpu.make_async_copy(three_hbm, b_v, load_sem.at[1])
    load_t = pltpu.make_async_copy(amps_hbm, t_v, load_sem.at[2])
    load_a.start()
    load_b.start()
    load_t.start()

    barrier = pltpu.get_barrier_semaphore()
    for device in (side(0), side(1), level(0), level(1)):
        pl.semaphore_signal(barrier, inc=1, device_id=device, device_id_type=MESH)
    pl.semaphore_wait(barrier, 4)

    order = (near, 1 - near)
    for d in order:
        for message in meta(d):
            message.start()
    for h in range(2):
        for d in order:
            xmsg(d, h).start()

    second = lax.rem(occ_ref[r, 1] - 2 * (c - 1) + 2 * n, 2 * n)
    where_j = jnp.minimum(second // 2, 2)
    i_at = lax.rem(occ_ref[r, 0], 2)
    j_at = lax.rem(occ_ref[r, 1], 2)
    occ_shift = eo_ref[occ_ref[r, 0]] + eo_ref[occ_ref[r, 1]]
    count = nv_ref[r]

    def weights(parts, coups):
        out = []
        for q in range(roles):
            total = jnp.float32(0.0)
            for k in range(part_ref.shape[1]):
                total = total + jnp.where(parts(k) == roles * c + q, coups(k), jnp.float32(0.0))
            out.append(total)
        return out

    def overlap(x, at):
        xt = x.T
        for q in range(roles):
            s_v[at, :, q * nv:(q + 1) * nv] = (dot(xt, a_v[q]) * (1.0 / npao)).astype(BF)

    def coupled(at, w, amp):
        for q in range(roles):
            u_v[:, q * nv:(q + 1) * nv] = (dot(s_v[at, :, q * nv:(q + 1) * nv], amp(q)) * w[q]).astype(BF)
        return dot_nt(u_v[...], s_v[at])

    rows = lax.broadcasted_iota(jnp.int32, (nv, nv), 0)
    cols = lax.broadcasted_iota(jnp.int32, (nv, nv), 1)
    ev = jnp.broadcast_to(ev_ref[pl.ds(r, 1), :], (nv, nv))
    keep = (rows < count) & (cols < count)
    rm_v[...] = jnp.where(keep, 1.0 / (ev + ev.T - occ_shift + 1.0), 0.0)
    w_own = weights(lambda k: part_ref[r, k], lambda k: coup_ref[r, k])

    load_a.wait()
    load_b.wait()
    own = a_v[r]
    yit_v[...] = (dot(b_v[i_at], own) * pao_scale).astype(BF).T
    yj = (dot(b_v[j_at], own) * pao_scale).astype(BF)
    for h in range(2):
        y_in[h][1] = yj[:, h * hw:(h + 1) * hw]
    load_t.wait()
    overlap(own, 2)
    c_own[...] = coupled(2, w_own, lambda q: t_v[q])

    for h in range(2):
        for d in order:
            if h == 0:
                for message in meta(1 - d):
                    message.wait_recv()
            xmsg(1 - d, h).wait_recv()
            j_near = lax.rem(occ_in[d, r, 1], 2)
            y_out[d, h] = (dot(b_v[j_near], x_in[d, :, h * hw:(h + 1) * hw]) * pao_scale).astype(BF)
            if h == 0:
                ymsg(d, h).start()
    w_near = []
    for d in order:
        w = weights(lambda k: part_in[d, r, k], lambda k: coup_in[d, r, k])
        w_near.append(w)
        overlap(x_in[d], d)
        c_out[d] = coupled(d, w, lambda q: t_v[q]).astype(BF)
        cmsg(d).start()
        ymsg(d, 1).start()

    for d in range(2):
        cmsg(d).wait_recv()
    for h in range(2):
        for d in range(2):
            ymsg(d, h).wait_recv()
        lanes = slice(h * hw, (h + 1) * hw)
        k1 = dot(yit_v[...], y_in[h][where_j]) * aux_scale
        k_v[:, lanes] = k1
        total = k1 + c_own[:, lanes] + c_in[0, :, lanes].astype(F32) + c_in[1, :, lanes].astype(F32)
        fresh = rm_v[:, lanes] * (t_v[r, :, lanes].astype(F32) - total)
        t1_v[r, h] = fresh.astype(BF)
        for v in range(2):
            direct(t1_v, T1D, v, h).start()
        t1_f[:, lanes] = fresh

    def whole(buf, at):
        return jnp.concatenate([buf[at, 0], buf[at, 1]], axis=1)

    t1 = t1_f[...].astype(BF)
    half = k_v[...] + dot(k_v[...].astype(BF), t1) * virt_scale
    k2 = half + dot(t1.T, half.astype(BF)) * virt_scale
    k_v[...] = t1_f[...] - k2

    for h in range(2):
        for v in range(2):
            direct(t1_v, T1D, 1 - v, h).wait_recv()
            forward(t1_v, T1F, 1 - v, h).start()
    for h in range(2):
        for v in range(2):
            forward(t1_v, T1F, v, h).wait_recv()

    for at, d in enumerate(order):
        part = coupled(d, w_near[at], lambda q: whole(t1_v, q)).astype(BF)
        for h in range(2):
            c2_out[d, h] = part[:, h * hw:(h + 1) * hw]
            c2msg(d, h).start()
    k_v[...] = k_v[...] - coupled(2, w_own, lambda q: whole(t1_v, q))

    for h in range(2):
        for d in range(2):
            c2msg(d, h).wait_recv()
        lanes = slice(h * hw, (h + 1) * hw)
        total = k_v[:, lanes] - c2_in[0, h].astype(F32) - c2_in[1, h].astype(F32)
        t2_v[r, h] = (rm_v[:, lanes] * total).astype(BF)
        for v in range(2):
            direct(t2_v, T2D, v, h).start()

    slots = []
    for s in range(SLOTS):
        pair, found = jnp.int32(0), jnp.int32(0)
        for q in range(roles):
            rank = jnp.int32(0)
            for e in range(q):
                rank = rank + jnp.where(own_ref[e] == own_ref[q], 1, 0)
            hit = jnp.where((own_ref[q] == r) & (rank == s), 1, 0)
            pair = pair + q * hit
            found = found + hit
        slots.append((pair, found.astype(F32)))

    for h in range(2):
        for v in range(2):
            direct(t2_v, T2D, 1 - v, h).wait_recv()
            forward(t2_v, T2F, 1 - v, h).start()
    for h in range(2):
        for v in range(2):
            forward(t2_v, T2F, v, h).wait_recv()
    for s, (pair, found) in enumerate(slots):
        amp = whole(t2_v, pair)
        out_amp[s] = (amp.astype(F32) * found).astype(BF)
        orb = a_v[pair]
        out_orb[s] = ((orb.astype(F32) + dot(orb, amp) * virt_scale) * found).astype(BF)

    for d in range(2):
        for message in meta(d):
            message.wait_send()
        cmsg(d).wait_send()
        for h in range(2):
            xmsg(d, h).wait_send()
            ymsg(d, h).wait_send()
            c2msg(d, h).wait_send()
            for buf, base, again in ((t1_v, T1D, T1F), (t2_v, T2D, T2F)):
                direct(buf, base, d, h).wait_send()
                forward(buf, again, d, h).wait_send()


def local(three_index, coeff, amps, eps_virt, eps_occ, nvirt, pair_occ, partners, coupling, pair_owner):
    n, roles = lax.axis_size("pairs"), lax.axis_size("role")
    _, naux, npao = three_index.shape
    pairs, _, nv = coeff.shape
    anywhere = pl.BlockSpec(memory_space=pl.ANY)
    scalars = pl.BlockSpec(memory_space=pltpu.SMEM)
    vector = pl.BlockSpec(memory_space=pltpu.VMEM)
    hw = nv // 2
    return pl.pallas_call(
        functools.partial(kernel, n, roles),
        out_shape=(
            jax.ShapeDtypeStruct((SLOTS, nv, nv), BF),
            jax.ShapeDtypeStruct((SLOTS, npao, nv), BF),
        ),
        in_specs=[anywhere] * 6 + [vector] + [scalars] * 6,
        out_specs=(vector, vector),
        scratch_shapes=[
            pltpu.VMEM(three_index.shape, BF),
            pltpu.VMEM(coeff.shape, BF),
            pltpu.VMEM(amps.shape, BF),
            pltpu.VMEM((2, npao, nv), BF),
            pltpu.VMEM((2, 2, naux, hw), BF),
            pltpu.VMEM((3, naux, hw), BF),
            pltpu.VMEM((3, naux, hw), BF),
            pltpu.VMEM((nv, naux), BF),
            pltpu.VMEM((3, nv, pairs * nv), BF),
            pltpu.VMEM((nv, pairs * nv), BF),
            pltpu.VMEM((2, nv, nv), BF),
            pltpu.VMEM((2, nv, nv), BF),
            pltpu.VMEM((nv, nv), F32),
            pltpu.VMEM((nv, nv), F32),
            pltpu.VMEM((nv, nv), F32),
            pltpu.VMEM((pairs, 2, nv, hw), BF),
            pltpu.VMEM((nv, nv), F32),
            pltpu.VMEM((2, 2, nv, hw), BF),
            pltpu.VMEM((2, 2, nv, hw), BF),
            pltpu.VMEM((pairs, 2, nv, hw), BF),
            pltpu.SMEM((2,) + pair_occ.shape, jnp.int32),
            pltpu.SMEM((2,) + partners.shape, jnp.int32),
            pltpu.SMEM((2,) + coupling.shape, F32),
            pltpu.SemaphoreType.DMA((3,)),
            pltpu.SemaphoreType.DMA((COUNT,)),
            pltpu.SemaphoreType.DMA((COUNT,)),
        ],
        compiler_params=pltpu.CompilerParams(
            collective_id=0, has_side_effects=True, vmem_limit_bytes=48 * 1024 * 1024
        ),
    )(
        three_index, coeff, amps, pair_occ, partners, coupling,
        eps_virt, eps_occ, nvirt, pair_occ, partners, coupling, pair_owner,
    )


def solution(mesh):
    in_specs = (
        P("pairs", None, None),
        P("pairs", None, None),
        P("pairs", None, None),
        P("pairs", None),
        P(),
        P("pairs"),
        P("pairs", None),
        P("pairs", None),
        P("pairs", None),
        P("pairs"),
    )
    out_specs = (P(("role", "pairs"), None, None), P(("role", "pairs"), None, None))
    return jax.shard_map(local, mesh=mesh, in_specs=in_specs, out_specs=out_specs, check_vma=False)
```

```python
import functools
import math

import jax
import jax.numpy as jnp
from jax import lax
from jax.experimental import pallas as pl
from jax.experimental.pallas import tpu as pltpu
from jax.sharding import PartitionSpec as P

SLOTS = 2
MESH = pl.DeviceIdType.MESH
BF = jnp.bfloat16
F32 = jnp.float32

OCC, PART, COUP, XM, CM, C2M, T1F, T2F, YM, T1D, T2D, COUNT = 0, 2, 4, 6, 10, 12, 16, 20, 24, 32, 40, 48


def dot(a, b):
    return jnp.dot(a, b, preferred_element_type=F32)


def dot_nt(a, b):
    return lax.dot_general(a, b, (((1,), (1,)), ((), ())), preferred_element_type=F32)


def kernel(
    n, roles,
    three_hbm, coeff_hbm, amps_hbm, occ_hbm, part_hbm, coup_hbm,
    ev_hbm, eo_hbm, nv_hbm, own_hbm,
    out_amp, out_orb,
    b_v, a_v, t_v, x_in, y_out, y_left, y_right, yit_v, s_v, u_v, c_out, c_in, c_own, rm_v, k_v,
    t1_v, t1_f, c2_out, c2_in, t2_v,
    occ_in, part_in, coup_in, w_v,
    ev_ref, eo_ref, nv_ref, occ_ref, part_ref, coup_ref, own_ref,
    load_sem, send_sem, recv_sem,
):
    r = lax.axis_index("role")
    c = lax.axis_index("pairs")
    up, down = lax.rem(r + 1, roles), lax.rem(r + roles - 1, roles)
    naux, npao = b_v.shape[1], b_v.shape[2]
    nv = a_v.shape[2]
    hw = nv // 2
    hr = nv // 2
    pao_scale = 1.0 / math.sqrt(npao)
    aux_scale = 1.0 / math.sqrt(naux)
    virt_scale = 1.0 / math.sqrt(nv)
    y_in = (y_left, y_right)
    near = lax.rem(c, 2)

    def remote(src, dst, base, s_at, r_at, device):
        return pltpu.make_async_remote_copy(
            src_ref=src, dst_ref=dst,
            send_sem=send_sem.at[base + s_at], recv_sem=recv_sem.at[base + r_at],
            device_id=device, device_id_type=MESH,
        )

    def side(d):
        return (r, lax.rem(c + 2 * d - 1 + n, n))

    def level(v):
        return (lax.rem(r + 1 + 2 * v, roles), c)

    def meta(d):
        return (
            remote(occ_hbm, occ_in.at[1 - d], OCC, d, 1 - d, side(d)),
            remote(part_hbm, part_in.at[1 - d], PART, d, 1 - d, side(d)),
            remote(coup_hbm, coup_in.at[1 - d], COUP, d, 1 - d, side(d)),
        )

    def xmsg(d, h):
        cols = pl.ds(h * hw, hw)
        return remote(coeff_hbm.at[r, :, cols], x_in.at[1 - d, :, cols], XM, 2 * d + h, 2 * (1 - d) + h, side(d))

    def ymsg(d, h, k):
        part = pl.ds(k * (naux // 2), naux // 2)
        return remote(
            y_out.at[d, h, part], y_in[h].at[2 * (1 - d), part],
            YM, 4 * d + 2 * h + k, 4 * (1 - d) + 2 * h + k, side(d),
        )

    def cmsg(d):
        return remote(c_out.at[d], c_in.at[1 - d], CM, d, 1 - d, side(d))

    def c2msg(d, h):
        return remote(c2_out.at[d, h], c2_in.at[1 - d, h], C2M, 2 * d + h, 2 * (1 - d) + h, side(d))

    def direct(buf, base, v, h, k):
        part = buf.at[r, h, pl.ds(k * hr, hr)]
        return remote(part, part, base, 4 * v + 2 * h + k, 4 * (1 - v) + 2 * h + k, level(v))

    def forward(buf, base, v, h):
        which = down if v == 0 else up
        part = buf.at[which, h, pl.ds(v * hr, hr)]
        return remote(part, part, base, 2 * v + h, 2 * (1 - v) + h, level(v))

    def spread(buf, base, h):
        for at in range(2):
            for v in range(2):
                direct(buf, base, v, h, v if at == 0 else 1 - v).start()

    def relay(buf, base, again, h):
        for v in range(2):
            direct(buf, base, 1 - v, h, 1 - v).wait_recv()
            forward(buf, again, 1 - v, h).start()

    barrier = pltpu.get_barrier_semaphore()
    for device in (side(0), side(1), level(0), level(1)):
        pl.semaphore_signal(barrier, inc=1, device_id=device, device_id_type=MESH)
    sources = (
        coeff_hbm, three_hbm, amps_hbm, occ_hbm, part_hbm, coup_hbm, ev_hbm, eo_hbm, nv_hbm, own_hbm
    )
    places = (a_v, b_v, t_v, occ_ref, part_ref, coup_ref, ev_ref, eo_ref, nv_ref, own_ref)
    loads = [
        pltpu.make_async_copy(src, dst, load_sem.at[at])
        for at, (src, dst) in enumerate(zip(sources, places))
    ]
    for load in loads[3:] + loads[:3]:
        load.start()
    pl.semaphore_wait(barrier, 4)

    order = (near, 1 - near)
    for d in order:
        meta(d)[0].start()
        xmsg(d, 0).start()
    for d in order:
        for message in meta(d)[1:]:
            message.start()
        xmsg(d, 1).start()

    for load in loads[3:]:
        load.wait()
    second = lax.rem(occ_ref[1, r] - 2 * (c - 1) + 2 * n, 2 * n)
    where_j = jnp.minimum(second // 2, 2)
    i_at = lax.rem(occ_ref[0, r], 2)
    j_at = lax.rem(occ_ref[1, r], 2)
    occ_shift = eo_ref[occ_ref[0, r]] + eo_ref[occ_ref[1, r]]
    count = nv_ref[r]

    def weights(at, parts, coups):
        for q in range(roles):
            total = jnp.float32(0.0)
            for k in range(part_ref.shape[1]):
                total = total + jnp.where(parts(k) == roles * c + q, coups(k), jnp.float32(0.0))
            w_v[at, q] = total

    def overlap(x, at):
        xt = x.T
        for q in range(roles):
            s_v[at, :, q * nv:(q + 1) * nv] = (dot(xt, a_v[q]) * (1.0 / npao)).astype(BF)

    def middle(at, q, amp):
        cols = pl.ds(pl.multiple_of(q * nv, nv), nv)
        u_v[at, :, cols] = (dot(s_v[at, :, cols], amp) * w_v[at, q]).astype(BF)

    def coupled(at):
        return dot_nt(u_v[at], s_v[at])

    def whole(buf, at):
        return jnp.concatenate([buf[at, 0], buf[at, 1]], axis=1)

    rows = lax.broadcasted_iota(jnp.int32, (nv, nv), 0)
    cols = lax.broadcasted_iota(jnp.int32, (nv, nv), 1)
    ev = jnp.broadcast_to(ev_ref[pl.ds(r, 1), :], (nv, nv))
    keep = (rows < count) & (cols < count)
    rm_v[...] = jnp.where(keep, 1.0 / (ev + ev.T - occ_shift + 1.0), 0.0)
    weights(2, lambda k: part_ref[r, k], lambda k: coup_ref[r, k])

    loads[0].wait()
    loads[1].wait()
    own = a_v[r]
    yit_v[...] = (dot(b_v[i_at], own) * pao_scale).astype(BF).T
    loads[2].wait()
    for d in order:
        meta(1 - d)[0].wait_recv()

    far = 1 - near
    half_aux = naux // 2
    near_at = lax.rem(occ_in[near, 1, r], 2)
    far_at = lax.rem(occ_in[far, 1, r], 2)

    def near_half(h):
        x = x_in[near, :, h * hw:(h + 1) * hw]
        for k in range(2):
            part = slice(k * half_aux, (k + 1) * half_aux)
            y_out[near, h, part] = (dot(b_v[near_at, part], x) * pao_scale).astype(BF)
            ymsg(near, h, k).start()

    xmsg(1 - near, 0).wait_recv()
    near_half(0)
    for h in range(2):
        xmsg(1 - far, h).wait_recv()
    y_far = (dot(b_v[far_at], x_in[far]) * pao_scale).astype(BF)
    for h in range(2):
        y_out[far, h] = y_far[:, h * hw:(h + 1) * hw]
    for h in range(2):
        for k in range(2):
            ymsg(far, h, k).start()
    xmsg(1 - near, 1).wait_recv()
    overlap(x_in[near], near)
    for at in (near, far):
        for message in meta(1 - at)[1:]:
            message.wait_recv()
        weights(at, lambda k: part_in[at, r, k], lambda k: coup_in[at, r, k])
        for q in range(roles):
            middle(at, q, t_v[q])
        c_out[at] = coupled(at).astype(BF)
        cmsg(at).start()
        if at is near:
            near_half(1)
            overlap(x_in[far], far)

    yj = (dot(b_v[j_at], own) * pao_scale).astype(BF)
    for h in range(2):
        y_in[h][1] = yj[:, h * hw:(h + 1) * hw]
    overlap(own, 2)
    for q in range(roles):
        middle(2, q, t_v[q])
    c_own[...] = t_v[r].astype(F32) - coupled(2)

    for h in range(2):
        for d in range(2):
            for k in range(2):
                ymsg(d, h, k).wait_recv()
        lanes = slice(h * hw, (h + 1) * hw)
        k1 = dot(yit_v[...], y_in[h][where_j]) * aux_scale
        k_v[:, lanes] = k1
        if h == 0:
            for d in range(2):
                cmsg(d).wait_recv()
            c_own[...] = c_own[...] - c_in[0].astype(F32) - c_in[1].astype(F32)
        fresh = rm_v[:, lanes] * (c_own[:, lanes] - k1)
        t1_v[r, h] = fresh.astype(BF)
        spread(t1_v, T1D, h)
        t1_f[:, lanes] = fresh
    relay(t1_v, T1D, T1F, 0)

    t1 = t1_f[...].astype(BF)
    for at in (near, far, 2):
        middle(at, r, t1)
    half = k_v[...] + dot(k_v[...].astype(BF), t1) * virt_scale
    k2 = half + dot(t1.T, half.astype(BF)) * virt_scale
    k_v[...] = t1_f[...] - k2

    relay(t1_v, T1D, T1F, 1)
    for v in range(2):
        for h in range(2):
            direct(t1_v, T1D, 1 - v, h, v).wait_recv()
    for q in (down, up):
        amp = whole(t1_v, q)
        for at in (near, far, 2):
            middle(at, q, amp)
    for h in range(2):
        for v in range(2):
            forward(t1_v, T1F, v, h).wait_recv()
    across = lax.rem(r + 2, roles)
    amp = whole(t1_v, across)
    for at in (near, far):
        middle(at, across, amp)
        part = coupled(at).astype(BF)
        for h in range(2):
            c2_out[at, h] = part[:, h * hw:(h + 1) * hw]
            c2msg(at, h).start()
    middle(2, across, amp)
    k_v[...] = k_v[...] - coupled(2)

    slots = []
    for s in range(SLOTS):
        pair, found = jnp.int32(0), jnp.int32(0)
        for q in range(roles):
            rank = jnp.int32(0)
            for e in range(q):
                rank = rank + jnp.where(own_ref[e] == own_ref[q], 1, 0)
            hit = jnp.where((own_ref[q] == r) & (rank == s), 1, 0)
            pair = pair + q * hit
            found = found + hit
        slots.append((pair, found.astype(F32)))

    for h in range(2):
        for d in range(2):
            c2msg(d, h).wait_recv()
        lanes = slice(h * hw, (h + 1) * hw)
        total = k_v[:, lanes] - c2_in[0, h].astype(F32) - c2_in[1, h].astype(F32)
        t2_v[r, h] = (rm_v[:, lanes] * total).astype(BF)
        spread(t2_v, T2D, h)
    for h in range(2):
        relay(t2_v, T2D, T2F, h)
    for h in range(2):
        for v in range(2):
            direct(t2_v, T2D, 1 - v, h, v).wait_recv()
    for h in range(2):
        for v in range(2):
            forward(t2_v, T2F, v, h).wait_recv()
    for s, (pair, found) in enumerate(slots):
        amp = whole(t2_v, pair)
        out_amp[s] = (amp.astype(F32) * found).astype(BF)
        orb = a_v[pair]
        out_orb[s] = ((orb.astype(F32) + dot(orb, amp) * virt_scale) * found).astype(BF)

    for d in range(2):
        for message in meta(d):
            message.wait_send()
        cmsg(d).wait_send()
        for h in range(2):
            xmsg(d, h).wait_send()
            c2msg(d, h).wait_send()
            for k in range(2):
                ymsg(d, h, k).wait_send()
            for buf, base, again in ((t1_v, T1D, T1F), (t2_v, T2D, T2F)):
                for k in range(2):
                    direct(buf, base, d, h, k).wait_send()
                forward(buf, again, d, h).wait_send()


def local(three_index, coeff, amps, eps_virt, eps_occ, nvirt, pair_occ, partners, coupling, pair_owner):
    n, roles = lax.axis_size("pairs"), lax.axis_size("role")
    _, naux, npao = three_index.shape
    pairs, _, nv = coeff.shape
    anywhere = pl.BlockSpec(memory_space=pl.ANY)
    vector = pl.BlockSpec(memory_space=pltpu.VMEM)
    hw = nv // 2
    return pl.pallas_call(
        functools.partial(kernel, n, roles),
        out_shape=(
            pltpu.VMEM((SLOTS, nv, nv), BF),
            pltpu.VMEM((SLOTS, npao, nv), BF),
        ),
        in_specs=[anywhere] * 10,
        out_specs=(vector, vector),
        scratch_shapes=[
            pltpu.VMEM(three_index.shape, BF),
            pltpu.VMEM(coeff.shape, BF),
            pltpu.VMEM(amps.shape, BF),
            pltpu.VMEM((2, npao, nv), BF),
            pltpu.VMEM((2, 2, naux, hw), BF),
            pltpu.VMEM((3, naux, hw), BF),
            pltpu.VMEM((3, naux, hw), BF),
            pltpu.VMEM((nv, naux), BF),
            pltpu.VMEM((3, nv, pairs * nv), BF),
            pltpu.VMEM((3, nv, pairs * nv), BF),
            pltpu.VMEM((2, nv, nv), BF),
            pltpu.VMEM((2, nv, nv), BF),
            pltpu.VMEM((nv, nv), F32),
            pltpu.VMEM((nv, nv), F32),
            pltpu.VMEM((nv, nv), F32),
            pltpu.VMEM((pairs, 2, nv, hw), BF),
            pltpu.VMEM((nv, nv), F32),
            pltpu.VMEM((2, 2, nv, hw), BF),
            pltpu.VMEM((2, 2, nv, hw), BF),
            pltpu.VMEM((pairs, 2, nv, hw), BF),
            pltpu.SMEM((2,) + pair_occ.shape[::-1], jnp.int32),
            pltpu.SMEM((2,) + partners.shape, jnp.int32),
            pltpu.SMEM((2,) + coupling.shape, F32),
            pltpu.SMEM((3, pairs), F32),
            pltpu.VMEM(eps_virt.shape, F32),
            pltpu.SMEM(eps_occ.shape, F32),
            pltpu.SMEM(nvirt.shape, jnp.int32),
            pltpu.SMEM(pair_occ.shape[::-1], jnp.int32),
            pltpu.SMEM(partners.shape, jnp.int32),
            pltpu.SMEM(coupling.shape, F32),
            pltpu.SMEM(pair_owner.shape, jnp.int32),
            pltpu.SemaphoreType.DMA((10,)),
            pltpu.SemaphoreType.DMA((COUNT,)),
            pltpu.SemaphoreType.DMA((COUNT,)),
        ],
        compiler_params=pltpu.CompilerParams(
            collective_id=0, has_side_effects=True, vmem_limit_bytes=64 * 1024 * 1024 - 2 * 1024 * 1024
        ),
    )(
        three_index, coeff, amps, pair_occ.T, partners, coupling,
        eps_virt, eps_occ, nvirt, pair_owner,
    )


def solution(mesh):
    in_specs = (
        P("pairs", None, None),
        P("pairs", None, None),
        P("pairs", None, None),
        P("pairs", None),
        P(),
        P("pairs"),
        P("pairs", None),
        P("pairs", None),
        P("pairs", None),
        P("pairs"),
    )
    out_specs = (P(("role", "pairs"), None, None), P(("role", "pairs"), None, None))
    return jax.shard_map(local, mesh=mesh, in_specs=in_specs, out_specs=out_specs, check_vma=False)
```

```python
import functools
import math

import jax
import jax.numpy as jnp
from jax import lax
from jax.experimental import pallas as pl
from jax.experimental.pallas import tpu as pltpu
from jax.sharding import PartitionSpec as P

SLOTS = 2
MESH = pl.DeviceIdType.MESH
BF = jnp.bfloat16
F32 = jnp.float32

OCC, PART, COUP, XM, CM, C2M, YM, T1D, T2D, BM, COUNT = 0, 2, 4, 6, 10, 12, 16, 24, 30, 36, 38


def dot(a, b):
    return jnp.dot(a, b, preferred_element_type=F32)


def dot_nt(a, b):
    return lax.dot_general(a, b, (((1,), (1,)), ((), ())), preferred_element_type=F32)


def kernel(
    n, roles,
    three_hbm, coeff_hbm, amps_hbm, occ_hbm, part_hbm, coup_hbm,
    ev_hbm, eo_hbm, nv_hbm, own_hbm,
    out_amp, out_orb,
    b_v, a_v, t_v, b_in, x_in, y_out, y_left, y_right, yit_v, s_v, u_v, c_out, c_in, c_own, rm_v, k_v,
    t1_v, t1_f, c2_out, c2_in, t2_v,
    occ_in, part_in, coup_in, w_v,
    ev_ref, eo_ref, nv_ref, occ_ref, part_ref, coup_ref, own_ref,
    load_sem, send_sem, recv_sem,
):
    r = lax.axis_index("role")
    c = lax.axis_index("pairs")
    turn = [lax.rem(r + step, roles) for step in (0, 1, 3, 2)]
    naux, npao = b_v.shape[1], b_v.shape[2]
    nv = a_v.shape[2]
    hw = nv // 2
    raw = naux // 8
    half_aux = (naux - raw) // 2
    pao_scale = 1.0 / math.sqrt(npao)
    aux_scale = 1.0 / math.sqrt(naux)
    virt_scale = 1.0 / math.sqrt(nv)
    y_in = (y_left, y_right)
    near = lax.rem(c, 2)

    def remote(src, dst, base, s_at, r_at, device):
        return pltpu.make_async_remote_copy(
            src_ref=src, dst_ref=dst,
            send_sem=send_sem.at[base + s_at], recv_sem=recv_sem.at[base + r_at],
            device_id=device, device_id_type=MESH,
        )

    def side(d):
        return (r, lax.rem(c + 2 * d - 1 + n, n))

    def level(v):
        return (lax.rem(r + 1 + v, roles), c)

    def meta(d):
        return (
            remote(occ_ref, occ_in.at[1 - d], OCC, d, 1 - d, side(d)),
            remote(part_ref, part_in.at[1 - d], PART, d, 1 - d, side(d)),
            remote(coup_ref, coup_in.at[1 - d], COUP, d, 1 - d, side(d)),
        )

    def xmsg(d, h):
        cols = pl.ds(h * hw, hw)
        return remote(a_v.at[r, :, cols], x_in.at[1 - d, :, cols], XM, 2 * d + h, 2 * (1 - d) + h, side(d))

    def bmsg(d):
        return remote(b_v.at[:, pl.ds(0, raw)], b_in.at[1 - d], BM, d, 1 - d, side(d))

    def ymsg(d, h, k):
        part = pl.ds(raw + k * half_aux, half_aux)
        return remote(
            y_out.at[d, h, part], y_in[h].at[2 * (1 - d), part],
            YM, 4 * d + 2 * h + k, 4 * (1 - d) + 2 * h + k, side(d),
        )

    def cmsg(d):
        return remote(c_out.at[d], c_in.at[1 - d], CM, d, 1 - d, side(d))

    def c2msg(d, h):
        return remote(c2_out.at[d, h], c2_in.at[1 - d, h], C2M, 2 * d + h, 2 * (1 - d) + h, side(d))

    def direct(buf, base, v, h):
        return remote(buf.at[r, h], buf.at[r, h], base, 2 * v + h, 2 * (2 - v) + h, level(v))

    def spread(buf, base, h):
        for v in (1, 0, 2):
            direct(buf, base, v, h).start()

    barrier = pltpu.get_barrier_semaphore()
    for device in (side(near), side(1 - near), level(0), level(1), level(2)):
        pl.semaphore_signal(barrier, inc=1, device_id=device, device_id_type=MESH)
    sources = (
        coeff_hbm, three_hbm, amps_hbm, occ_hbm, part_hbm, coup_hbm, ev_hbm, eo_hbm, nv_hbm, own_hbm
    )
    places = (a_v, b_v, t_v, occ_ref, part_ref, coup_ref, ev_ref, eo_ref, nv_ref, own_ref)
    loads = [
        pltpu.make_async_copy(src, dst, load_sem.at[at])
        for at, (src, dst) in enumerate(zip(sources, places))
    ]
    for load in loads[3:] + loads[:3]:
        load.start()
    pl.semaphore_wait(barrier, 5)

    order = (near, 1 - near)
    for load in loads[3:] + loads[:1]:
        load.wait()
    for d in order:
        meta(d)[0].start()
        xmsg(d, 0).start()
    for d in order:
        for message in meta(d)[1:]:
            message.start()
        xmsg(d, 1).start()
    loads[1].wait()
    for d in order:
        bmsg(d).start()

    second = lax.rem(occ_ref[1, r] - 2 * (c - 1) + 2 * n, 2 * n)
    where_j = jnp.minimum(second // 2, 2)
    i_at = lax.rem(occ_ref[0, r], 2)
    j_at = lax.rem(occ_ref[1, r], 2)
    occ_shift = eo_ref[occ_ref[0, r]] + eo_ref[occ_ref[1, r]]
    count = nv_ref[r]

    def weights(at, parts, coups):
        for q in range(roles):
            total = jnp.float32(0.0)
            for k in range(part_ref.shape[1]):
                total = total + jnp.where(parts(k) == roles * c + q, coups(k), jnp.float32(0.0))
            w_v[at, q] = total

    def overlap(x, at):
        xt = x.T
        for k, q in enumerate(turn):
            s_v[at, :, k * nv:(k + 1) * nv] = (dot(xt, a_v[q]) * (1.0 / npao)).astype(BF)

    def middle(at, k, amp):
        lanes = slice(k * nv, (k + 1) * nv)
        u_v[at, :, lanes] = (dot(s_v[at, :, lanes], amp) * w_v[at, turn[k]]).astype(BF)

    def coupled(at, first=0, last=roles):
        lanes = slice(first * nv, last * nv)
        return dot_nt(u_v[at, :, lanes], s_v[at, :, lanes])

    def whole(buf, at):
        return jnp.concatenate([buf[at, 0], buf[at, 1]], axis=1)

    rows = lax.broadcasted_iota(jnp.int32, (nv, nv), 0)
    cols = lax.broadcasted_iota(jnp.int32, (nv, nv), 1)
    ev = jnp.broadcast_to(ev_ref[pl.ds(r, 1), :], (nv, nv))
    keep = (rows < count) & (cols < count)
    rm_v[...] = jnp.where(keep, 1.0 / (ev + ev.T - occ_shift + 1.0), 0.0)
    weights(2, lambda k: part_ref[r, k], lambda k: coup_ref[r, k])

    own = a_v[r]
    yit_v[...] = (dot(b_v[i_at], own) * pao_scale).astype(BF).T
    loads[2].wait()
    for d in order:
        meta(1 - d)[0].wait_recv()

    far = 1 - near
    near_at = lax.rem(occ_in[near, 1, r], 2)
    far_at = lax.rem(occ_in[far, 1, r], 2)

    def near_half(h):
        x = x_in[near, :, h * hw:(h + 1) * hw]
        for k in range(2):
            part = slice(raw + k * half_aux, raw + (k + 1) * half_aux)
            y_out[near, h, part] = (dot(b_v[near_at, part], x) * pao_scale).astype(BF)
            ymsg(near, h, k).start()

    xmsg(1 - near, 0).wait_recv()
    near_half(0)
    for h in range(2):
        xmsg(1 - far, h).wait_recv()
    y_far = (dot(b_v[far_at, raw:], x_in[far]) * pao_scale).astype(BF)
    for h in range(2):
        y_out[far, h, raw:] = y_far[:, h * hw:(h + 1) * hw]
    for h in range(2):
        for k in range(2):
            ymsg(far, h, k).start()
    xmsg(1 - near, 1).wait_recv()
    overlap(x_in[near], near)
    for at in (near, far):
        for message in meta(1 - at)[1:]:
            message.wait_recv()
        weights(at, lambda k: part_in[at, r, k], lambda k: coup_in[at, r, k])
        for k, q in enumerate(turn):
            middle(at, k, t_v[q])
        c_out[at] = coupled(at).astype(BF)
        cmsg(at).start()
        if at is near:
            near_half(1)
            overlap(x_in[far], far)

    yj = (dot(b_v[j_at], own) * pao_scale).astype(BF)
    for h in range(2):
        y_in[h][1] = yj[:, h * hw:(h + 1) * hw]
    for d in range(2):
        bmsg(d).wait_recv()
    for d in range(2):
        yb = (dot(b_in[d, j_at], own) * pao_scale).astype(BF)
        for h in range(2):
            y_in[h][2 * d, :raw] = yb[:, h * hw:(h + 1) * hw]
    overlap(own, 2)
    for k, q in enumerate(turn):
        middle(2, k, t_v[q])
    c_own[...] = t_v[r].astype(F32) - coupled(2)

    for h in range(2):
        for d in range(2):
            for k in range(2):
                ymsg(d, h, k).wait_recv()
        lanes = slice(h * hw, (h + 1) * hw)
        k1 = dot(yit_v[...], y_in[h][where_j]) * aux_scale
        k_v[:, lanes] = k1
        if h == 0:
            for d in range(2):
                cmsg(d).wait_recv()
            c_own[...] = c_own[...] - c_in[0].astype(F32) - c_in[1].astype(F32)
        fresh = rm_v[:, lanes] * (c_own[:, lanes] - k1)
        t1_v[r, h] = fresh.astype(BF)
        spread(t1_v, T1D, h)
        t1_f[:, lanes] = fresh

    t1 = t1_f[...].astype(BF)
    for at in (near, far, 2):
        middle(at, 0, t1)
    half = k_v[...] + dot(k_v[...].astype(BF), t1) * virt_scale
    k2 = half + dot(t1.T, half.astype(BF)) * virt_scale
    k_v[...] = t1_f[...] - k2

    def arrived(buf, base, k):
        for h in range(2):
            direct(buf, base, (None, 2, 0, 1)[k], h).wait_recv()

    def send_c2(at, part):
        for h in range(2):
            c2_out[at, h] = part[:, h * hw:(h + 1) * hw].astype(BF)
            c2msg(at, h).start()

    for k in (1, 2):
        arrived(t1_v, T1D, k)
        middle(near, k, whole(t1_v, turn[k]))
    t1_f[...] = coupled(near, 0, 3)
    arrived(t1_v, T1D, 3)
    middle(near, 3, whole(t1_v, turn[3]))
    send_c2(near, t1_f[...] + coupled(near, 3, 4))
    for k in (1, 2, 3):
        middle(far, k, whole(t1_v, turn[k]))
    send_c2(far, coupled(far))
    for k in (1, 2, 3):
        middle(2, k, whole(t1_v, turn[k]))
    k_v[...] = k_v[...] - coupled(2)

    for d in range(2):
        for message in meta(d):
            message.wait_send()
        cmsg(d).wait_send()
        bmsg(d).wait_send()
        for h in range(2):
            xmsg(d, h).wait_send()
            for k in range(2):
                ymsg(d, h, k).wait_send()
    for v in range(3):
        for h in range(2):
            direct(t1_v, T1D, v, h).wait_send()

    slots = []
    for s in range(SLOTS):
        pair, found = jnp.int32(0), jnp.int32(0)
        for q in range(roles):
            rank = jnp.int32(0)
            for e in range(q):
                rank = rank + jnp.where(own_ref[e] == own_ref[q], 1, 0)
            hit = jnp.where((own_ref[q] == r) & (rank == s), 1, 0)
            pair = pair + q * hit
            found = found + hit
        slots.append((pair, found.astype(F32)))

    for h in range(2):
        for d in range(2):
            c2msg(d, h).wait_recv()
        lanes = slice(h * hw, (h + 1) * hw)
        total = k_v[:, lanes] - c2_in[0, h].astype(F32) - c2_in[1, h].astype(F32)
        t2_v[r, h] = (rm_v[:, lanes] * total).astype(BF)
        spread(t2_v, T2D, h)
    for k in (1, 2, 3):
        arrived(t2_v, T2D, k)
    for s, (pair, found) in enumerate(slots):
        amp = whole(t2_v, pair)
        out_amp[s] = (amp.astype(F32) * found).astype(BF)
        orb = a_v[pair]
        out_orb[s] = ((orb.astype(F32) + dot(orb, amp) * virt_scale) * found).astype(BF)

    for h in range(2):
        for d in range(2):
            c2msg(d, h).wait_send()
        for v in range(3):
            direct(t2_v, T2D, v, h).wait_send()


def local(three_index, coeff, amps, eps_virt, eps_occ, nvirt, pair_occ, partners, coupling, pair_owner):
    n, roles = lax.axis_size("pairs"), lax.axis_size("role")
    _, naux, npao = three_index.shape
    pairs, _, nv = coeff.shape
    anywhere = pl.BlockSpec(memory_space=pl.ANY)
    vector = pl.BlockSpec(memory_space=pltpu.VMEM)
    hw = nv // 2
    return pl.pallas_call(
        functools.partial(kernel, n, roles),
        out_shape=(
            pltpu.VMEM((SLOTS, nv, nv), BF),
            pltpu.VMEM((SLOTS, npao, nv), BF),
        ),
        in_specs=[anywhere] * 10,
        out_specs=(vector, vector),
        scratch_shapes=[
            pltpu.VMEM(three_index.shape, BF),
            pltpu.VMEM(coeff.shape, BF),
            pltpu.VMEM(amps.shape, BF),
            pltpu.VMEM((2, 2, naux // 8, npao), BF),
            pltpu.VMEM((2, npao, nv), BF),
            pltpu.VMEM((2, 2, naux, hw), BF),
            pltpu.VMEM((3, naux, hw), BF),
            pltpu.VMEM((3, naux, hw), BF),
            pltpu.VMEM((nv, naux), BF),
            pltpu.VMEM((3, nv, pairs * nv), BF),
            pltpu.VMEM((3, nv, pairs * nv), BF),
            pltpu.VMEM((2, nv, nv), BF),
            pltpu.VMEM((2, nv, nv), BF),
            pltpu.VMEM((nv, nv), F32),
            pltpu.VMEM((nv, nv), F32),
            pltpu.VMEM((nv, nv), F32),
            pltpu.VMEM((pairs, 2, nv, hw), BF),
            pltpu.VMEM((nv, nv), F32),
            pltpu.VMEM((2, 2, nv, hw), BF),
            pltpu.VMEM((2, 2, nv, hw), BF),
            pltpu.VMEM((pairs, 2, nv, hw), BF),
            pltpu.SMEM((2,) + pair_occ.shape[::-1], jnp.int32),
            pltpu.SMEM((2,) + partners.shape, jnp.int32),
            pltpu.SMEM((2,) + coupling.shape, F32),
            pltpu.SMEM((3, pairs), F32),
            pltpu.VMEM(eps_virt.shape, F32),
            pltpu.SMEM(eps_occ.shape, F32),
            pltpu.SMEM(nvirt.shape, jnp.int32),
            pltpu.SMEM(pair_occ.shape[::-1], jnp.int32),
            pltpu.SMEM(partners.shape, jnp.int32),
            pltpu.SMEM(coupling.shape, F32),
            pltpu.SMEM(pair_owner.shape, jnp.int32),
            pltpu.SemaphoreType.DMA((10,)),
            pltpu.SemaphoreType.DMA((COUNT,)),
            pltpu.SemaphoreType.DMA((COUNT,)),
        ],
        compiler_params=pltpu.CompilerParams(
            collective_id=0, has_side_effects=True, vmem_limit_bytes=64 * 1024 * 1024 - 2 * 1024 * 1024
        ),
    )(
        three_index, coeff, amps, pair_occ.T, partners, coupling,
        eps_virt, eps_occ, nvirt, pair_owner,
    )


def solution(mesh):
    in_specs = (
        P("pairs", None, None),
        P("pairs", None, None),
        P("pairs", None, None),
        P("pairs", None),
        P(),
        P("pairs"),
        P("pairs", None),
        P("pairs", None),
        P("pairs", None),
        P("pairs"),
    )
    out_specs = (P(("role", "pairs"), None, None), P(("role", "pairs"), None, None))
    return jax.shard_map(local, mesh=mesh, in_specs=in_specs, out_specs=out_specs, check_vma=False)
```

```python
import functools
import math

import jax
import jax.numpy as jnp
from jax import lax
from jax.experimental import pallas as pl
from jax.experimental.pallas import tpu as pltpu
from jax.sharding import PartitionSpec as P

SLOTS = 2
MESH = pl.DeviceIdType.MESH
BF = jnp.bfloat16
F32 = jnp.float32

OCC, PART, COUP, XM, CM, C2M, YM, T1D, T2D, BM, OWN, COUNT = 0, 2, 4, 6, 10, 12, 16, 24, 30, 36, 38, 40


def dot(a, b):
    return jnp.dot(a, b, preferred_element_type=F32)


def dot_nt(a, b):
    return lax.dot_general(a, b, (((1,), (1,)), ((), ())), preferred_element_type=F32)


def kernel(
    n, roles,
    three_hbm, coeff_hbm, amps_hbm, occ_hbm, part_hbm, coup_hbm,
    ev_hbm, eo_hbm, nv_hbm, own_hbm,
    out_amp, out_orb,
    b_v, a_v, t_v, b_in, x_in, y_out, y_left, y_right, yit_v, s_v, u_v, c_out, c_in, c_own, rm_v, k_v,
    t1_v, t1_f, c2_out, c2_in, t2_out, t2_in, x_out,
    occ_in, part_in, coup_in, own_in, w_v,
    ev_ref, eo_ref, nv_ref, occ_ref, part_ref, coup_ref, own_ref,
    load_sem, send_sem, recv_sem,
):
    r = lax.axis_index("role")
    c = lax.axis_index("pairs")
    turn = [lax.rem(r + step, roles) for step in (0, 1, 3, 2)]
    naux, npao = b_v.shape[1], b_v.shape[2]
    nv = a_v.shape[2]
    hw = nv // 2
    raw = naux // 8
    half_aux = (naux - raw) // 2
    pao_scale = 1.0 / math.sqrt(npao)
    aux_scale = 1.0 / math.sqrt(naux)
    virt_scale = 1.0 / math.sqrt(nv)
    y_in = (y_left, y_right)
    near = lax.rem(c, 2)

    def remote(src, dst, base, s_at, r_at, device):
        return pltpu.make_async_remote_copy(
            src_ref=src, dst_ref=dst,
            send_sem=send_sem.at[base + s_at], recv_sem=recv_sem.at[base + r_at],
            device_id=device, device_id_type=MESH,
        )

    def side(d):
        return (r, lax.rem(c + 2 * d - 1 + n, n))

    def level(v):
        return (lax.rem(r + 1 + v, roles), c)

    def meta(d):
        return (
            remote(occ_ref, occ_in.at[1 - d], OCC, d, 1 - d, side(d)),
            remote(part_ref, part_in.at[1 - d], PART, d, 1 - d, side(d)),
            remote(coup_ref, coup_in.at[1 - d], COUP, d, 1 - d, side(d)),
            remote(own_ref, own_in.at[1 - d], OWN, d, 1 - d, side(d)),
        )

    def xmsg(d, h):
        cols = pl.ds(h * hw, hw)
        return remote(x_out.at[:, cols], x_in.at[1 - d, :, cols], XM, 2 * d + h, 2 * (1 - d) + h, side(d))

    def bmsg(d):
        return remote(b_v.at[:, pl.ds(0, raw)], b_in.at[1 - d], BM, d, 1 - d, side(d))

    def ymsg(d, h, k):
        part = pl.ds(raw + k * half_aux, half_aux)
        return remote(
            y_out.at[d, h, part], y_in[h].at[2 * (1 - d), part],
            YM, 4 * d + 2 * h + k, 4 * (1 - d) + 2 * h + k, side(d),
        )

    def cmsg(d):
        return remote(c_out.at[d], c_in.at[1 - d], CM, d, 1 - d, side(d))

    def c2msg(d, h):
        return remote(c2_out.at[d, h], c2_in.at[1 - d, h], C2M, 2 * d + h, 2 * (1 - d) + h, side(d))

    def direct(buf, base, v, h):
        return remote(buf.at[r, h], buf.at[r, h], base, 2 * v + h, 2 * (2 - v) + h, level(v))

    def spread(buf, base, h):
        for v in (1, 0, 2):
            direct(buf, base, v, h).start()

    def last(v, h):
        return remote(t2_out.at[h], t2_in.at[h], T2D, 2 * v + h, h, level(v))

    def pair_of(owner, role):
        found = jnp.int32(0)
        for q in range(roles):
            rank = jnp.int32(0)
            for e in range(q):
                rank = rank + jnp.where(owner(e) == owner(q), 1, 0)
            first = (owner(q) == role) & (rank == 0) & (role > 0)
            found = found + jnp.where(first | ((role == 0) & (rank == 1)), q, 0)
        return found

    barrier = pltpu.get_barrier_semaphore()
    for device in (side(near), side(1 - near), level(0), level(1), level(2)):
        pl.semaphore_signal(barrier, inc=1, device_id=device, device_id_type=MESH)
    sources = (
        coeff_hbm, three_hbm, amps_hbm, occ_hbm, part_hbm, coup_hbm, ev_hbm, eo_hbm, nv_hbm, own_hbm
    )
    places = (a_v, b_v, t_v, occ_ref, part_ref, coup_ref, ev_ref, eo_ref, nv_ref, own_ref)
    loads = [
        pltpu.make_async_copy(src, dst, load_sem.at[at])
        for at, (src, dst) in enumerate(zip(sources, places))
    ]
    for load in loads[3:] + loads[:3]:
        load.start()
    for load in loads[3:] + loads[:1]:
        load.wait()
    pairs = [pair_of(lambda e: own_ref[e], role) for role in turn]
    mine = pairs[0]
    x_out[...] = a_v[mine]
    pl.semaphore_wait(barrier, 5)

    order = (near, 1 - near)
    for d in order:
        meta(d)[0].start()
        meta(d)[3].start()
        xmsg(d, 0).start()
    for d in order:
        for message in meta(d)[1:3]:
            message.start()
        xmsg(d, 1).start()
    loads[1].wait()
    for d in order:
        bmsg(d).start()

    second = lax.rem(occ_ref[1, mine] - 2 * (c - 1) + 2 * n, 2 * n)
    where_j = jnp.minimum(second // 2, 2)
    i_at = lax.rem(occ_ref[0, mine], 2)
    j_at = lax.rem(occ_ref[1, mine], 2)
    occ_shift = eo_ref[occ_ref[0, mine]] + eo_ref[occ_ref[1, mine]]
    count = nv_ref[mine]

    def weights(at, parts, coups):
        for q in range(roles):
            total = jnp.float32(0.0)
            for k in range(part_ref.shape[1]):
                total = total + jnp.where(parts(k) == roles * c + q, coups(k), jnp.float32(0.0))
            w_v[at, q] = total

    def overlap(x, at):
        xt = x.T
        for k, q in enumerate(pairs):
            s_v[at, :, k * nv:(k + 1) * nv] = (dot(xt, a_v[q]) * (1.0 / npao)).astype(BF)

    def middle(at, k, amp):
        lanes = slice(k * nv, (k + 1) * nv)
        u_v[at, :, lanes] = (dot(s_v[at, :, lanes], amp) * w_v[at, pairs[k]]).astype(BF)

    def coupled(at, first=0, last=roles):
        lanes = slice(first * nv, last * nv)
        return dot_nt(u_v[at, :, lanes], s_v[at, :, lanes])

    def whole(buf, at):
        return jnp.concatenate([buf[at, 0], buf[at, 1]], axis=1)

    rows = lax.broadcasted_iota(jnp.int32, (nv, nv), 0)
    cols = lax.broadcasted_iota(jnp.int32, (nv, nv), 1)
    ev = jnp.broadcast_to(ev_ref[pl.ds(mine, 1), :], (nv, nv))
    keep = (rows < count) & (cols < count)
    rm_v[...] = jnp.where(keep, 1.0 / (ev + ev.T - occ_shift + 1.0), 0.0)
    weights(2, lambda k: part_ref[mine, k], lambda k: coup_ref[mine, k])

    own = a_v[mine]
    yit_v[...] = (dot(b_v[i_at], own) * pao_scale).astype(BF).T
    loads[2].wait()
    for d in order:
        meta(1 - d)[0].wait_recv()
        meta(1 - d)[3].wait_recv()

    far = 1 - near
    near_pair = pair_of(lambda e: own_in[near, e], r)
    far_pair = pair_of(lambda e: own_in[far, e], r)
    near_at = lax.rem(occ_in[near, 1, near_pair], 2)
    far_at = lax.rem(occ_in[far, 1, far_pair], 2)

    def near_half(h):
        x = x_in[near, :, h * hw:(h + 1) * hw]
        for k in range(2):
            part = slice(raw + k * half_aux, raw + (k + 1) * half_aux)
            y_out[near, h, part] = (dot(b_v[near_at, part], x) * pao_scale).astype(BF)
            ymsg(near, h, k).start()

    xmsg(1 - near, 0).wait_recv()
    near_half(0)
    for h in range(2):
        xmsg(1 - far, h).wait_recv()
    y_far = (dot(b_v[far_at, raw:], x_in[far]) * pao_scale).astype(BF)
    for h in range(2):
        y_out[far, h, raw:] = y_far[:, h * hw:(h + 1) * hw]
    for h in range(2):
        for k in range(2):
            ymsg(far, h, k).start()
    xmsg(1 - near, 1).wait_recv()
    overlap(x_in[near], near)
    for d in order:
        for message in meta(1 - d)[1:3]:
            message.wait_recv()
    for at, pair in ((near, near_pair), (far, far_pair)):
        weights(at, lambda k: part_in[at, pair, k], lambda k: coup_in[at, pair, k])
        for k, q in enumerate(pairs):
            middle(at, k, t_v[q])
        c_out[at] = coupled(at).astype(BF)
        cmsg(at).start()
        if at is near:
            near_half(1)
            overlap(x_in[far], far)

    yj = (dot(b_v[j_at], own) * pao_scale).astype(BF)
    for h in range(2):
        y_in[h][1] = yj[:, h * hw:(h + 1) * hw]
    for d in range(2):
        bmsg(d).wait_recv()
    for d in range(2):
        yb = (dot(b_in[d, j_at], own) * pao_scale).astype(BF)
        for h in range(2):
            y_in[h][2 * d, :raw] = yb[:, h * hw:(h + 1) * hw]
    overlap(own, 2)
    for k, q in enumerate(pairs):
        middle(2, k, t_v[q])
    c_own[...] = t_v[mine].astype(F32) - coupled(2)

    for h in range(2):
        for d in range(2):
            for k in range(2):
                ymsg(d, h, k).wait_recv()
        lanes = slice(h * hw, (h + 1) * hw)
        k1 = dot(yit_v[...], y_in[h][where_j]) * aux_scale
        k_v[:, lanes] = k1
        if h == 0:
            for d in range(2):
                cmsg(d).wait_recv()
            c_own[...] = c_own[...] - c_in[0].astype(F32) - c_in[1].astype(F32)
        fresh = rm_v[:, lanes] * (c_own[:, lanes] - k1)
        t1_v[r, h] = fresh.astype(BF)
        spread(t1_v, T1D, h)
        t1_f[:, lanes] = fresh

    t1 = t1_f[...].astype(BF)
    for at in (near, far, 2):
        middle(at, 0, t1)
    half = k_v[...] + dot(k_v[...].astype(BF), t1) * virt_scale
    k2 = half + dot(t1.T, half.astype(BF)) * virt_scale
    k_v[...] = t1_f[...] - k2

    def arrived(buf, base, k):
        for h in range(2):
            direct(buf, base, (None, 2, 0, 1)[k], h).wait_recv()

    def send_c2(at, part):
        for h in range(2):
            c2_out[at, h] = part[:, h * hw:(h + 1) * hw].astype(BF)
            c2msg(at, h).start()

    for k in (1, 2):
        arrived(t1_v, T1D, k)
        middle(near, k, whole(t1_v, turn[k]))
    t1_f[...] = coupled(near, 0, 3)
    arrived(t1_v, T1D, 3)
    middle(near, 3, whole(t1_v, turn[3]))
    send_c2(near, t1_f[...] + coupled(near, 3, 4))
    for k in (1, 2, 3):
        middle(far, k, whole(t1_v, turn[k]))
    send_c2(far, coupled(far))
    for k in (1, 2, 3):
        middle(2, k, whole(t1_v, turn[k]))
    k_v[...] = k_v[...] - coupled(2)

    for d in range(2):
        for message in meta(d):
            message.wait_send()
        cmsg(d).wait_send()
        bmsg(d).wait_send()
        for h in range(2):
            xmsg(d, h).wait_send()
            for k in range(2):
                ymsg(d, h, k).wait_send()
    for v in range(3):
        for h in range(2):
            direct(t1_v, T1D, v, h).wait_send()

    for h in range(2):
        for d in range(2):
            c2msg(d, h).wait_recv()
        lanes = slice(h * hw, (h + 1) * hw)
        total = k_v[:, lanes] - c2_in[0, h].astype(F32) - c2_in[1, h].astype(F32)
        t2_out[h] = (rm_v[:, lanes] * total).astype(BF)

        @pl.when(r == 0)
        def _():
            for v in (1, 0, 2):
                last(v, h).start()

    def emit(slot, buf, pair, found):
        amp = jnp.concatenate([buf[0], buf[1]], axis=1)
        out_amp[slot] = (amp.astype(F32) * found).astype(BF)
        orb = a_v[pair]
        out_orb[slot] = ((orb.astype(F32) + dot(orb, amp) * virt_scale) * found).astype(BF)

    emit(0, t2_out, mine, jnp.where(r > 0, jnp.float32(1.0), jnp.float32(0.0)))
    second_pair = pair_of(lambda e: own_ref[e], jnp.int32(0))
    held = jnp.where(own_ref[second_pair] == r, jnp.float32(1.0), jnp.float32(0.0))

    @pl.when(r > 0)
    def _():
        for h in range(2):
            last(0, h).wait_recv()
        emit(1, t2_in, second_pair, held)

    @pl.when(r == 0)
    def _():
        out_amp[1] = jnp.zeros_like(out_amp[1])
        out_orb[1] = jnp.zeros_like(out_orb[1])
        for h in range(2):
            for v in range(3):
                last(v, h).wait_send()

    for h in range(2):
        for d in range(2):
            c2msg(d, h).wait_send()


def local(three_index, coeff, amps, eps_virt, eps_occ, nvirt, pair_occ, partners, coupling, pair_owner):
    n, roles = lax.axis_size("pairs"), lax.axis_size("role")
    _, naux, npao = three_index.shape
    pairs, _, nv = coeff.shape
    anywhere = pl.BlockSpec(memory_space=pl.ANY)
    vector = pl.BlockSpec(memory_space=pltpu.VMEM)
    hw = nv // 2
    return pl.pallas_call(
        functools.partial(kernel, n, roles),
        out_shape=(
            pltpu.VMEM((SLOTS, nv, nv), BF),
            pltpu.VMEM((SLOTS, npao, nv), BF),
        ),
        in_specs=[anywhere] * 10,
        out_specs=(vector, vector),
        scratch_shapes=[
            pltpu.VMEM(three_index.shape, BF),
            pltpu.VMEM(coeff.shape, BF),
            pltpu.VMEM(amps.shape, BF),
            pltpu.VMEM((2, 2, naux // 8, npao), BF),
            pltpu.VMEM((2, npao, nv), BF),
            pltpu.VMEM((2, 2, naux, hw), BF),
            pltpu.VMEM((3, naux, hw), BF),
            pltpu.VMEM((3, naux, hw), BF),
            pltpu.VMEM((nv, naux), BF),
            pltpu.VMEM((3, nv, pairs * nv), BF),
            pltpu.VMEM((3, nv, pairs * nv), BF),
            pltpu.VMEM((2, nv, nv), BF),
            pltpu.VMEM((2, nv, nv), BF),
            pltpu.VMEM((nv, nv), F32),
            pltpu.VMEM((nv, nv), F32),
            pltpu.VMEM((nv, nv), F32),
            pltpu.VMEM((pairs, 2, nv, hw), BF),
            pltpu.VMEM((nv, nv), F32),
            pltpu.VMEM((2, 2, nv, hw), BF),
            pltpu.VMEM((2, 2, nv, hw), BF),
            pltpu.VMEM((2, nv, hw), BF),
            pltpu.VMEM((2, nv, hw), BF),
            pltpu.VMEM((npao, nv), BF),
            pltpu.SMEM((2,) + pair_occ.shape[::-1], jnp.int32),
            pltpu.SMEM((2,) + partners.shape, jnp.int32),
            pltpu.SMEM((2,) + coupling.shape, F32),
            pltpu.SMEM((2,) + pair_owner.shape, jnp.int32),
            pltpu.SMEM((3, pairs), F32),
            pltpu.VMEM(eps_virt.shape, F32),
            pltpu.SMEM(eps_occ.shape, F32),
            pltpu.SMEM(nvirt.shape, jnp.int32),
            pltpu.SMEM(pair_occ.shape[::-1], jnp.int32),
            pltpu.SMEM(partners.shape, jnp.int32),
            pltpu.SMEM(coupling.shape, F32),
            pltpu.SMEM(pair_owner.shape, jnp.int32),
            pltpu.SemaphoreType.DMA((10,)),
            pltpu.SemaphoreType.DMA((COUNT,)),
            pltpu.SemaphoreType.DMA((COUNT,)),
        ],
        compiler_params=pltpu.CompilerParams(
            collective_id=0, has_side_effects=True, vmem_limit_bytes=64 * 1024 * 1024 - 2 * 1024 * 1024
        ),
    )(
        three_index, coeff, amps, pair_occ.T, partners, coupling,
        eps_virt, eps_occ, nvirt, pair_owner,
    )


def solution(mesh):
    in_specs = (
        P("pairs", None, None),
        P("pairs", None, None),
        P("pairs", None, None),
        P("pairs", None),
        P(),
        P("pairs"),
        P("pairs", None),
        P("pairs", None),
        P("pairs", None),
        P("pairs"),
    )
    out_specs = (P(("role", "pairs"), None, None), P(("role", "pairs"), None, None))
    return jax.shard_map(local, mesh=mesh, in_specs=in_specs, out_specs=out_specs, check_vma=False)
```

```python
import functools
import math

import jax
import jax.numpy as jnp
from jax import lax
from jax.experimental import pallas as pl
from jax.experimental.pallas import tpu as pltpu
from jax.sharding import PartitionSpec as P

SLOTS = 2
MESH = pl.DeviceIdType.MESH
BF = jnp.bfloat16
F32 = jnp.float32

OCC, PART, COUP, XM, CM, C2M, YM, T1D, T2D, BM, OWN, COUNT = 0, 2, 4, 6, 10, 12, 16, 24, 30, 36, 38, 40


def dot(a, b):
    return jnp.dot(a, b, preferred_element_type=F32)


def dot_nt(a, b):
    return lax.dot_general(a, b, (((1,), (1,)), ((), ())), preferred_element_type=F32)


def kernel(
    n, roles,
    three_hbm, coeff_hbm, amps_hbm, occ_hbm, part_hbm, coup_hbm,
    ev_hbm, eo_hbm, nv_hbm, own_hbm,
    out_amp, out_orb,
    b_v, a_v, t_v, b_in, x_in, y_out, y_left, y_right, yit_v, s_v, u_v, c_out, c_in, c_own, rm_v, k_v,
    t1_v, t1_f, c2_out, c2_in, t2_out, t2_in, x_out,
    occ_in, part_in, coup_in, own_in, w_v,
    ev_ref, eo_ref, nv_ref, occ_ref, part_ref, coup_ref, own_ref,
    load_sem, send_sem, recv_sem,
):
    r = lax.axis_index("role")
    c = lax.axis_index("pairs")
    turn = [lax.rem(r + step, roles) for step in (0, 1, 3, 2)]
    naux, npao = b_v.shape[1], b_v.shape[2]
    nv = a_v.shape[2]
    hw = nv // 2
    raw = naux // 16
    half_aux = (naux - raw) // 2
    pao_scale = 1.0 / math.sqrt(npao)
    aux_scale = 1.0 / math.sqrt(naux)
    virt_scale = 1.0 / math.sqrt(nv)
    y_in = (y_left, y_right)
    near = lax.rem(c, 2)

    def remote(src, dst, base, s_at, r_at, device):
        return pltpu.make_async_remote_copy(
            src_ref=src, dst_ref=dst,
            send_sem=send_sem.at[base + s_at], recv_sem=recv_sem.at[base + r_at],
            device_id=device, device_id_type=MESH,
        )

    def side(d):
        return (r, lax.rem(c + 2 * d - 1 + n, n))

    def level(v):
        return (lax.rem(r + 1 + v, roles), c)

    def meta(d):
        return (
            remote(occ_ref, occ_in.at[1 - d], OCC, d, 1 - d, side(d)),
            remote(part_ref, part_in.at[1 - d], PART, d, 1 - d, side(d)),
            remote(coup_ref, coup_in.at[1 - d], COUP, d, 1 - d, side(d)),
            remote(own_ref, own_in.at[1 - d], OWN, d, 1 - d, side(d)),
        )

    def xmsg(d, h):
        cols = pl.ds(h * hw, hw)
        return remote(x_out.at[:, cols], x_in.at[1 - d, :, cols], XM, 2 * d + h, 2 * (1 - d) + h, side(d))

    def bmsg(d):
        return remote(b_v.at[:, pl.ds(0, raw)], b_in.at[1 - d], BM, d, 1 - d, side(d))

    def ymsg(d, h, k):
        part = pl.ds(raw + k * half_aux, half_aux)
        return remote(
            y_out.at[d, h, part], y_in[h].at[2 * (1 - d), part],
            YM, 4 * d + 2 * h + k, 4 * (1 - d) + 2 * h + k, side(d),
        )

    def cmsg(d):
        return remote(c_out.at[d], c_in.at[1 - d], CM, d, 1 - d, side(d))

    def c2msg(d, h):
        return remote(c2_out.at[d, h], c2_in.at[1 - d, h], C2M, 2 * d + h, 2 * (1 - d) + h, side(d))

    def direct(buf, base, v, h):
        return remote(buf.at[r, h], buf.at[r, h], base, 2 * v + h, 2 * (2 - v) + h, level(v))

    def spread(buf, base, h):
        for v in (1, 0, 2):
            direct(buf, base, v, h).start()

    def last(v, h):
        return remote(t2_out.at[h], t2_in.at[h], T2D, 2 * v + h, h, level(v))

    def pair_of(owner, role):
        found = jnp.int32(0)
        for q in range(roles):
            rank = jnp.int32(0)
            for e in range(q):
                rank = rank + jnp.where(owner(e) == owner(q), 1, 0)
            first = (owner(q) == role) & (rank == 0) & (role > 0)
            found = found + jnp.where(first | ((role == 0) & (rank == 1)), q, 0)
        return found

    barrier = pltpu.get_barrier_semaphore()
    for device in (side(near), side(1 - near), level(0), level(1), level(2)):
        pl.semaphore_signal(barrier, inc=1, device_id=device, device_id_type=MESH)
    sources = (
        coeff_hbm, three_hbm, amps_hbm, occ_hbm, part_hbm, coup_hbm, ev_hbm, eo_hbm, nv_hbm, own_hbm
    )
    places = (a_v, b_v, t_v, occ_ref, part_ref, coup_ref, ev_ref, eo_ref, nv_ref, own_ref)
    loads = [
        pltpu.make_async_copy(src, dst, load_sem.at[at])
        for at, (src, dst) in enumerate(zip(sources, places))
    ]
    for load in loads[3:] + loads[:3]:
        load.start()
    for load in loads[3:] + loads[:1]:
        load.wait()
    pairs = [pair_of(lambda e: own_ref[e], role) for role in turn]
    mine = pairs[0]
    x_out[...] = a_v[mine]
    pl.semaphore_wait(barrier, 5)

    order = (near, 1 - near)
    for d in order:
        meta(d)[0].start()
        meta(d)[3].start()
        xmsg(d, 0).start()
    for d in order:
        for message in meta(d)[1:3]:
            message.start()
        xmsg(d, 1).start()
    loads[1].wait()
    for d in order:
        bmsg(d).start()

    second = lax.rem(occ_ref[1, mine] - 2 * (c - 1) + 2 * n, 2 * n)
    where_j = jnp.minimum(second // 2, 2)
    i_at = lax.rem(occ_ref[0, mine], 2)
    j_at = lax.rem(occ_ref[1, mine], 2)
    occ_shift = eo_ref[occ_ref[0, mine]] + eo_ref[occ_ref[1, mine]]
    count = nv_ref[mine]

    def weights(at, parts, coups):
        for q in range(roles):
            total = jnp.float32(0.0)
            for k in range(part_ref.shape[1]):
                total = total + jnp.where(parts(k) == roles * c + q, coups(k), jnp.float32(0.0))
            w_v[at, q] = total

    def overlap(x, at):
        xt = x.T
        for k, q in enumerate(pairs):
            s_v[at, :, k * nv:(k + 1) * nv] = (dot(xt, a_v[q]) * (1.0 / npao)).astype(BF)

    def middle(at, k, amp):
        lanes = slice(k * nv, (k + 1) * nv)
        u_v[at, :, lanes] = (dot(s_v[at, :, lanes], amp) * w_v[at, pairs[k]]).astype(BF)

    def coupled(at, first=0, last=roles):
        lanes = slice(first * nv, last * nv)
        return dot_nt(u_v[at, :, lanes], s_v[at, :, lanes])

    def whole(buf, at):
        return jnp.concatenate([buf[at, 0], buf[at, 1]], axis=1)

    rows = lax.broadcasted_iota(jnp.int32, (nv, nv), 0)
    cols = lax.broadcasted_iota(jnp.int32, (nv, nv), 1)
    ev = jnp.broadcast_to(ev_ref[pl.ds(mine, 1), :], (nv, nv))
    keep = (rows < count) & (cols < count)
    rm_v[...] = jnp.where(keep, 1.0 / (ev + ev.T - occ_shift + 1.0), 0.0)
    weights(2, lambda k: part_ref[mine, k], lambda k: coup_ref[mine, k])

    own = a_v[mine]
    yit_v[...] = (dot(b_v[i_at], own) * pao_scale).astype(BF).T
    loads[2].wait()
    for d in order:
        meta(1 - d)[0].wait_recv()
        meta(1 - d)[3].wait_recv()

    far = 1 - near
    near_pair = pair_of(lambda e: own_in[near, e], r)
    far_pair = pair_of(lambda e: own_in[far, e], r)
    near_at = lax.rem(occ_in[near, 1, near_pair], 2)
    far_at = lax.rem(occ_in[far, 1, far_pair], 2)

    def near_half(h):
        x = x_in[near, :, h * hw:(h + 1) * hw]
        for k in range(2):
            part = slice(raw + k * half_aux, raw + (k + 1) * half_aux)
            y_out[near, h, part] = (dot(b_v[near_at, part], x) * pao_scale).astype(BF)
            ymsg(near, h, k).start()

    xmsg(1 - near, 0).wait_recv()
    near_half(0)
    for h in range(2):
        xmsg(1 - far, h).wait_recv()
    y_far = (dot(b_v[far_at, raw:], x_in[far]) * pao_scale).astype(BF)
    for h in range(2):
        y_out[far, h, raw:] = y_far[:, h * hw:(h + 1) * hw]
    for h in range(2):
        for k in range(2):
            ymsg(far, h, k).start()
    xmsg(1 - near, 1).wait_recv()
    overlap(x_in[near], near)
    for d in order:
        for message in meta(1 - d)[1:3]:
            message.wait_recv()
    for at, pair in ((near, near_pair), (far, far_pair)):
        weights(at, lambda k: part_in[at, pair, k], lambda k: coup_in[at, pair, k])
        for k, q in enumerate(pairs):
            middle(at, k, t_v[q])
        c_out[at] = coupled(at).astype(BF)
        cmsg(at).start()
        if at is near:
            near_half(1)
            overlap(x_in[far], far)

    yj = (dot(b_v[j_at], own) * pao_scale).astype(BF)
    for h in range(2):
        y_in[h][1] = yj[:, h * hw:(h + 1) * hw]
    for d in range(2):
        bmsg(d).wait_recv()
    for d in range(2):
        yb = (dot(b_in[d, j_at], own) * pao_scale).astype(BF)
        for h in range(2):
            y_in[h][2 * d, :raw] = yb[:, h * hw:(h + 1) * hw]
    overlap(own, 2)
    for k, q in enumerate(pairs):
        middle(2, k, t_v[q])
    c_own[...] = t_v[mine].astype(F32) - coupled(2)

    for h in range(2):
        for d in range(2):
            for k in range(2):
                ymsg(d, h, k).wait_recv()
        lanes = slice(h * hw, (h + 1) * hw)
        k1 = dot(yit_v[...], y_in[h][where_j]) * aux_scale
        k_v[:, lanes] = k1
        if h == 0:
            for d in range(2):
                cmsg(d).wait_recv()
            c_own[...] = c_own[...] - c_in[0].astype(F32) - c_in[1].astype(F32)
        fresh = rm_v[:, lanes] * (c_own[:, lanes] - k1)
        t1_v[r, h] = fresh.astype(BF)
        spread(t1_v, T1D, h)
        t1_f[:, lanes] = fresh

    t1 = t1_f[...].astype(BF)
    for at in (near, far, 2):
        middle(at, 0, t1)
    half = k_v[...] + dot(k_v[...].astype(BF), t1) * virt_scale
    k2 = half + dot(t1.T, half.astype(BF)) * virt_scale
    k_v[...] = t1_f[...] - k2

    def arrived(buf, base, k):
        for h in range(2):
            direct(buf, base, (None, 2, 0, 1)[k], h).wait_recv()

    def send_c2(at, part):
        for h in range(2):
            c2_out[at, h] = part[:, h * hw:(h + 1) * hw].astype(BF)
            c2msg(at, h).start()

    for k in (1, 2):
        arrived(t1_v, T1D, k)
        middle(near, k, whole(t1_v, turn[k]))
    t1_f[...] = coupled(near, 0, 3)
    arrived(t1_v, T1D, 3)
    middle(near, 3, whole(t1_v, turn[3]))
    send_c2(near, t1_f[...] + coupled(near, 3, 4))
    for k in (1, 2, 3):
        middle(far, k, whole(t1_v, turn[k]))
    send_c2(far, coupled(far))
    for k in (1, 2, 3):
        middle(2, k, whole(t1_v, turn[k]))
    k_v[...] = k_v[...] - coupled(2)

    for d in range(2):
        for message in meta(d):
            message.wait_send()
        cmsg(d).wait_send()
        bmsg(d).wait_send()
        for h in range(2):
            xmsg(d, h).wait_send()
            for k in range(2):
                ymsg(d, h, k).wait_send()
    for v in range(3):
        for h in range(2):
            direct(t1_v, T1D, v, h).wait_send()

    for h in range(2):
        for d in range(2):
            c2msg(d, h).wait_recv()
        lanes = slice(h * hw, (h + 1) * hw)
        total = k_v[:, lanes] - c2_in[0, h].astype(F32) - c2_in[1, h].astype(F32)
        t2_out[h] = (rm_v[:, lanes] * total).astype(BF)

        @pl.when(r == 0)
        def _():
            for v in (1, 0, 2):
                last(v, h).start()

    def emit(slot, buf, pair, found):
        amp = jnp.concatenate([buf[0], buf[1]], axis=1)
        out_amp[slot] = (amp.astype(F32) * found).astype(BF)
        orb = a_v[pair]
        out_orb[slot] = ((orb.astype(F32) + dot(orb, amp) * virt_scale) * found).astype(BF)

    emit(0, t2_out, mine, jnp.where(r > 0, jnp.float32(1.0), jnp.float32(0.0)))
    second_pair = pair_of(lambda e: own_ref[e], jnp.int32(0))
    held = jnp.where(own_ref[second_pair] == r, jnp.float32(1.0), jnp.float32(0.0))

    @pl.when(r > 0)
    def _():
        for h in range(2):
            last(0, h).wait_recv()
        emit(1, t2_in, second_pair, held)

    @pl.when(r == 0)
    def _():
        out_amp[1] = jnp.zeros_like(out_amp[1])
        out_orb[1] = jnp.zeros_like(out_orb[1])
        for h in range(2):
            for v in range(3):
                last(v, h).wait_send()

    for h in range(2):
        for d in range(2):
            c2msg(d, h).wait_send()


def local(three_index, coeff, amps, eps_virt, eps_occ, nvirt, pair_occ, partners, coupling, pair_owner):
    n, roles = lax.axis_size("pairs"), lax.axis_size("role")
    _, naux, npao = three_index.shape
    pairs, _, nv = coeff.shape
    anywhere = pl.BlockSpec(memory_space=pl.ANY)
    vector = pl.BlockSpec(memory_space=pltpu.VMEM)
    hw = nv // 2
    return pl.pallas_call(
        functools.partial(kernel, n, roles),
        out_shape=(
            pltpu.VMEM((SLOTS, nv, nv), BF),
            pltpu.VMEM((SLOTS, npao, nv), BF),
        ),
        in_specs=[anywhere] * 10,
        out_specs=(vector, vector),
        scratch_shapes=[
            pltpu.VMEM(three_index.shape, BF),
            pltpu.VMEM(coeff.shape, BF),
            pltpu.VMEM(amps.shape, BF),
            pltpu.VMEM((2, 2, naux // 16, npao), BF),
            pltpu.VMEM((2, npao, nv), BF),
            pltpu.VMEM((2, 2, naux, hw), BF),
            pltpu.VMEM((3, naux, hw), BF),
            pltpu.VMEM((3, naux, hw), BF),
            pltpu.VMEM((nv, naux), BF),
            pltpu.VMEM((3, nv, pairs * nv), BF),
            pltpu.VMEM((3, nv, pairs * nv), BF),
            pltpu.VMEM((2, nv, nv), BF),
            pltpu.VMEM((2, nv, nv), BF),
            pltpu.VMEM((nv, nv), F32),
            pltpu.VMEM((nv, nv), F32),
            pltpu.VMEM((nv, nv), F32),
            pltpu.VMEM((pairs, 2, nv, hw), BF),
            pltpu.VMEM((nv, nv), F32),
            pltpu.VMEM((2, 2, nv, hw), BF),
            pltpu.VMEM((2, 2, nv, hw), BF),
            pltpu.VMEM((2, nv, hw), BF),
            pltpu.VMEM((2, nv, hw), BF),
            pltpu.VMEM((npao, nv), BF),
            pltpu.SMEM((2,) + pair_occ.shape[::-1], jnp.int32),
            pltpu.SMEM((2,) + partners.shape, jnp.int32),
            pltpu.SMEM((2,) + coupling.shape, F32),
            pltpu.SMEM((2,) + pair_owner.shape, jnp.int32),
            pltpu.SMEM((3, pairs), F32),
            pltpu.VMEM(eps_virt.shape, F32),
            pltpu.SMEM(eps_occ.shape, F32),
            pltpu.SMEM(nvirt.shape, jnp.int32),
            pltpu.SMEM(pair_occ.shape[::-1], jnp.int32),
            pltpu.SMEM(partners.shape, jnp.int32),
            pltpu.SMEM(coupling.shape, F32),
            pltpu.SMEM(pair_owner.shape, jnp.int32),
            pltpu.SemaphoreType.DMA((10,)),
            pltpu.SemaphoreType.DMA((COUNT,)),
            pltpu.SemaphoreType.DMA((COUNT,)),
        ],
        compiler_params=pltpu.CompilerParams(
            collective_id=0, has_side_effects=True, vmem_limit_bytes=64 * 1024 * 1024 - 2 * 1024 * 1024
        ),
    )(
        three_index, coeff, amps, pair_occ.T, partners, coupling,
        eps_virt, eps_occ, nvirt, pair_owner,
    )


def solution(mesh):
    in_specs = (
        P("pairs", None, None),
        P("pairs", None, None),
        P("pairs", None, None),
        P("pairs", None),
        P(),
        P("pairs"),
        P("pairs", None),
        P("pairs", None),
        P("pairs", None),
        P("pairs"),
    )
    out_specs = (P(("role", "pairs"), None, None), P(("role", "pairs"), None, None))
    return jax.shard_map(local, mesh=mesh, in_specs=in_specs, out_specs=out_specs, check_vma=False)
```
